512 devices in a mesh: tm: 64 (over z, y_hi, core), freq: 8 (over y_lo, x).
Axes of the slice: x: 4, y: 8 (y_hi: 4, y_lo: 2; y = y_hi * 2 + y_lo), z: 8, core: 2. Of those that a mesh axis runs over, the one named last changes fastest.
Arguments:
- spec: bfloat16 [256, 8192, 128], P('freq', 'tm')
- segment_ids: int32 [8192], replicated, may hold values from 0 to 63, never falling along the last dimension, each value on 1 to 256 neighbouring positions
- active: int32 [8192], replicated, may hold values 0 or 1
- time_gain: float32 [128], replicated, as said below
- time_match: bfloat16 [128, 128], replicated, may hold values from -0.5 to 0.5
- time_value: bfloat16 [128, 128], replicated, may hold values from -0.5 to 0.5
- time_out: bfloat16 [128, 128], replicated, may hold values from -0.5 to 0.5
- freq_gain: float32 [128], replicated, as said below
- freq_match: bfloat16 [128, 128], replicated, may hold values from -0.5 to 0.5
- freq_value: bfloat16 [128, 128], replicated, may hold values from -0.5 to 0.5
- freq_out: bfloat16 [128, 128], replicated, may hold values from -0.5 to 0.5
- mlp_gain: float32 [128], replicated, may hold values from 0.1 to 1.9
- mlp_up: bfloat16 [128, 512], replicated, may hold values from -0.5 to 0.5
- mlp_down: bfloat16 [512, 128], replicated, may hold values from -0.25 to 0.25
Outputs:
- block_out: bfloat16 [256, 8192, 128], P('freq', 'tm')
The draws below stay inside these ranges and needn't reach their ends.
Inputs may be any that keep to these rules, and one draw needn't show every extreme that they name: `segment_ids`: never falling along the frames; each recording spans 1 to 256 frames, one exactly that many. `time_gain`: positive. `freq_gain`: positive.
All inputs are finite; a program needn't handle non-finite values.
Results may differ from the reference program's by a relative error of at most 0.017.
The reference program's roundings to bfloat16 on the way count: a program that leaves them out, or rounds other values in their place, can miss the bound.
Values may be sent and summed in bfloat16 or wider, within the bound.
No kernel may reach another device: no remote copies, remote signals or barrier semaphores. Data moves between devices by JAX's collectives and lax.ppermute only.
A program may use at most 64 MiB of HBM per device.

```python
import math
import jax
import jax.numpy as jnp
import numpy as np
from jax import lax

BINS = 256
C = 128
HEADS = 4
HID = 512
TDEV = 128
HALO = 64
FRAMES = 8192
N_TM = 64


def draw_spec(key, part):
    first = jax.random.fold_in(jax.random.fold_in(key, 11), 0)
    base = jax.random.normal(first, (BINS, FRAMES, C), jnp.float32)
    return base.astype(jnp.bfloat16)


def head_gains(key):
    first = jax.random.fold_in(key, 0)
    jitter = jax.random.uniform(first, (C,), jnp.float32, 0.5, 1.5)
    return jitter


def draw_time_gain(key, part):
    return head_gains(jax.random.fold_in(key, 21)).astype(jnp.float32)


def draw_freq_gain(key, part):
    return head_gains(jax.random.fold_in(key, 31)).astype(jnp.float32)


def plant(entries, key, least, high):
    dims = entries.shape
    place = [jax.random.randint(jax.random.fold_in(key, axis), (), 0, dims[axis]) for axis in range(len(dims))]
    entries = entries.at[tuple(place)].set(least)
    longest = dims.index(max(dims))
    place[longest] = (place[longest] + 1) % dims[longest]
    return entries.at[tuple(place)].set(high)


def profile(count, total, limit, slope):
    portions = [(1 << 20) // math.isqrt(rank ** slope) + 1 for rank in range(2, count + 1)]
    rest, holding = total - limit - (count - 1), [1] * (count - 1)
    while rest > 0:
        movable = [i for i in range(count - 1) if holding[i] < limit]
        whole, left = sum([portions[i] for i in movable]), rest
        for i in movable:
            more = min(limit - holding[i], max(1, left * portions[i] // whole), rest)
            holding[i] = holding[i] + more
            rest = rest - more
    return np.array([limit] + holding)


def ragged(rng, number_of, total, limit, slope):
    if number_of == 2:
        one = jax.random.randint(rng, (), max(1, total - limit), min(limit, total - 1) + 1)
        return jnp.stack([one, total - one])
    sizes = jnp.asarray(profile(number_of, total, limit, slope), jnp.int32)
    pairs = (number_of - 1) // 2
    donor, sink = sizes[1:1 + 2 * pairs:2], sizes[2:2 + 2 * pairs:2]
    room = jnp.minimum(donor - 1, limit - sink)
    moved = jax.random.randint(jax.random.fold_in(rng, 1), (pairs,), 0, 1 << 20) % (room + 1)
    sizes = sizes.at[1:1 + 2 * pairs:2].set(donor - moved).at[2:2 + 2 * pairs:2].set(sink + moved)
    return sizes[jax.random.permutation(jax.random.fold_in(rng, 2), number_of)]


def noise(rng, shape, scale, reach, kind=jnp.bfloat16):
    result = jax.random.normal(rng, shape, jnp.float32) * scale
    return jnp.minimum(jnp.maximum(result, -reach), reach).astype(kind)


def setup_inputs(seed: int = 0) -> dict:
    key_of = jax.random.split(jax.random.key(seed), 15)
    return {
        "spec": draw_spec(jax.random.fold_in(key_of[14], 71), 0),
        "segment_ids": jnp.searchsorted(jnp.cumsum(ragged(key_of[1], N_TM, FRAMES, 2 * TDEV, 1)), jnp.arange(FRAMES), side="right").astype(jnp.int32),
        "active": plant((jax.random.randint(key_of[2], (FRAMES,), 0, 4) < 3).astype(jnp.int32), jax.random.fold_in(key_of[2], 1), 0, 1),
        "time_gain": draw_time_gain(jax.random.fold_in(key_of[14], 71), 0),
        "time_match": noise(key_of[4], (C, C), C ** -0.5, 0.5),
        "time_value": noise(key_of[5], (C, C), C ** -0.5, 0.5),
        "time_out": noise(key_of[6], (C, C), C ** -0.5, 0.5),
        "freq_gain": draw_freq_gain(jax.random.fold_in(key_of[14], 71), 0),
        "freq_match": noise(key_of[8], (C, C), C ** -0.5, 0.5),
        "freq_value": noise(key_of[9], (C, C), C ** -0.5, 0.5),
        "freq_out": noise(key_of[10], (C, C), C ** -0.5, 0.5),
        "mlp_gain": jnp.clip(1.0 + 0.18 * jax.random.normal(key_of[11], (C,), jnp.float32), 0.1, 1.9),
        "mlp_up": noise(key_of[12], (C, HID), C ** -0.5, 0.5),
        "mlp_down": noise(key_of[13], (HID, C), HID ** -0.5, 0.25),
    }


def layer_norm(values, gain):
    widened = values.astype(jnp.float32)
    centred = widened - lax.optimization_barrier(jnp.mean(widened, -1, keepdims=True))
    spread = lax.optimization_barrier(jnp.mean(centred * centred, -1, keepdims=True))
    return (centred * lax.rsqrt(spread + 1e-05) * gain).astype(jnp.bfloat16)

def project(values, weight):
    return jnp.dot(values, weight, preferred_element_type=jnp.float32).astype(jnp.bfloat16)

def add_branch(base, mixed, weight):
    return (base.astype(jnp.float32) + jnp.dot(mixed, weight, preferred_element_type=jnp.float32)).astype(jnp.bfloat16)

def attend(query, key_rows, value_rows, allowed):
    heads_q = query.reshape(query.shape[:-1] + (HEADS, -1)).astype(jnp.float32)
    heads_k = key_rows.reshape(key_rows.shape[:-1] + (HEADS, -1)).astype(jnp.float32)
    heads_v = value_rows.reshape(value_rows.shape[:-1] + (HEADS, -1)).astype(jnp.float32)
    scores = jnp.einsum('...thd,...shd->...hts', heads_q, heads_k) * heads_q.shape[-1] ** (-0.5)
    if allowed is not None:
        scores = jnp.where(allowed, scores, -1e+30)
    largest = lax.optimization_barrier(jnp.max(scores, -1, keepdims=True))
    weights = jnp.exp(scores - largest)
    shares = (weights / lax.optimization_barrier(jnp.sum(weights, -1, keepdims=True))).astype(jnp.bfloat16)
    mixed = jnp.einsum('...hts,...shd->...thd', shares.astype(jnp.float32), heads_v)
    return mixed.reshape(query.shape).astype(jnp.bfloat16)

def reference(spec, segment_ids, active, time_gain, time_match, time_value, time_out, freq_gain, freq_match, freq_value, freq_out, mlp_gain, mlp_up, mlp_down):
    bins, frames, width = spec.shape
    blocks = frames // TDEV
    normed = layer_norm(spec, time_gain)
    match_rows = project(normed, time_match)
    value_rows = project(normed, time_value)
    pad_match = jnp.pad(match_rows, ((0, 0), (HALO, HALO), (0, 0)))
    pad_value = jnp.pad(value_rows, ((0, 0), (HALO, HALO), (0, 0)))
    pad_segment = jnp.pad(segment_ids, HALO, constant_values=-1)
    pad_active = jnp.pad(active, HALO)
    span = TDEV + 2 * HALO

    def one_block(index):
        start = (index * TDEV).astype(jnp.int32)
        query = lax.dynamic_slice_in_dim(match_rows, start, TDEV, 1)
        key_rows = lax.dynamic_slice_in_dim(pad_match, start, span, 1)
        vals = lax.dynamic_slice_in_dim(pad_value, start, span, 1)
        seg_query = lax.dynamic_slice_in_dim(segment_ids, start, TDEV, 0)
        seg_key = lax.dynamic_slice_in_dim(pad_segment, start, span, 0)
        act_key = lax.dynamic_slice_in_dim(pad_active, start, span, 0)
        pos_query = start + jnp.arange(TDEV, dtype=jnp.int32)
        pos_key = start - HALO + jnp.arange(span, dtype=jnp.int32)
        inside = (pos_key >= 0) & (pos_key < frames)
        allowed = inside[None, :] & (seg_query[:, None] == seg_key[None, :]) & ((act_key[None, :] == 1) | (pos_query[:, None] == pos_key[None, :]))
        return attend(query, key_rows, vals, allowed)
    time_mix = lax.map(one_block, jnp.arange(blocks, dtype=jnp.int32))
    time_mix = jnp.transpose(time_mix, (1, 0, 2, 3)).reshape(bins, frames, width)
    after_time = add_branch(spec, time_mix, time_out)
    freq_normed = layer_norm(after_time, freq_gain)
    freq_keys = jnp.transpose(project(freq_normed, freq_match), (1, 0, 2)).reshape(blocks, TDEV, bins, width)
    freq_values = jnp.transpose(project(freq_normed, freq_value), (1, 0, 2)).reshape(blocks, TDEV, bins, width)

    def one_group(items):
        return attend(items[0], items[0], items[1], None)
    freq_mix = lax.map(one_group, (freq_keys, freq_values)).reshape(frames, bins, width)
    freq_mix = jnp.transpose(freq_mix, (1, 0, 2))
    after_freq = add_branch(after_time, freq_mix, freq_out)
    hidden = jax.nn.gelu(jnp.dot(layer_norm(after_freq, mlp_gain), mlp_up, preferred_element_type=jnp.float32)).astype(jnp.bfloat16)
    return add_branch(after_freq, hidden, mlp_down)
```

```python
import functools
import math

import jax
import jax.numpy as jnp
from jax import lax
from jax.experimental import pallas as pl
from jax.experimental.pallas import tpu as pltpu
from jax.sharding import PartitionSpec as P

HEADS = 4
HALO = 64
GROUP = 16
F32 = jnp.float32
BF16 = jnp.bfloat16
NEG = -1e30
ONES_ROWS = 16


def layer_norm(values, gain):
    widened = values.astype(F32)
    centred = widened - jnp.mean(widened, -1, keepdims=True)
    spread = jnp.mean(centred * centred, -1, keepdims=True)
    return (centred * lax.rsqrt(spread + 1e-05) * gain).astype(BF16)


def dot_nt(a, b):
    return lax.dot_general(a, b, (((1,), (1,)), ((), ())), preferred_element_type=F32)


def dot_tn(a, b):
    return lax.dot_general(a, b, (((0,), (0,)), ((), ())), preferred_element_type=F32)


def dot_nn(a, b):
    return jnp.dot(a, b, preferred_element_type=F32)


def head_scales(width):
    head = lax.broadcasted_iota(jnp.int32, (1, width), 1) // (width // HEADS)
    scale = (width // HEADS) ** (-0.5) * math.log2(math.e)
    return [jnp.where(head == h, scale, 0.0).astype(F32) for h in range(HEADS)]


def mix_heads(key_rows, query, values_t, scales, key_extra, query_extra):
    count = query.shape[0]
    width = query.shape[1] // HEADS
    wide = query.astype(F32)
    pieces = []
    for h in range(HEADS):
        side = (wide * scales[h]).astype(BF16)
        if query_extra is not None:
            side = jnp.concatenate([side, query_extra], 1)
        rows = key_rows if key_extra is None else jnp.concatenate([key_rows, key_extra], 1)
        scores = dot_nt(rows, side)
        weights = jnp.exp2(scores - jnp.max(scores, 0, keepdims=True)).astype(BF16)
        own = jnp.concatenate(
            [values_t[h * width : (h + 1) * width], jnp.ones((ONES_ROWS, values_t.shape[1]), BF16)], 0
        )
        mixed = dot_nn(own, weights)
        pieces.append(mixed[:width] / mixed[width : width + 1])
    return jnp.concatenate(pieces, 0)


def time_kernel(before, own, after, bias, eye, time_gain, match, value_t, out_w, freq_gain, after_time, sent, turned):
    scales = head_scales(own.shape[2])
    count = own.shape[1]

    def one_bin(b, carry):
        spec = own[b]
        joined = jnp.concatenate([before[b], spec, after[b]], 0)
        normed = layer_norm(joined, time_gain[...])
        key_rows = dot_nn(normed, match[...]).astype(BF16)
        values_t = dot_nt(value_t[...], normed).astype(BF16)
        mixed = mix_heads(key_rows, key_rows[HALO : HALO + count], values_t, scales, bias[...], eye[...])
        result = (spec.astype(F32) + dot_tn(mixed.astype(BF16), out_w[...])).astype(BF16)
        after_time[b] = result
        turned[pl.ds(b, count, stride=GROUP), :] = layer_norm(result, freq_gain[...]).astype(F32)
        return carry

    lax.fori_loop(0, GROUP, one_bin, 0, unroll=2)
    sent[...] = turned[...].reshape(count, GROUP, own.shape[2]).astype(BF16)


def freq_kernel(rows, match, value_t, mixed_out):
    parts, frames, each, width = rows.shape
    scales = head_scales(width)

    def one_frame(f, carry):
        normed = rows[:, f].reshape(parts * each, width)
        key_rows = dot_nn(normed, match[...]).astype(BF16)
        values_t = dot_nt(value_t[...], normed).astype(BF16)
        mixed = mix_heads(key_rows, key_rows, values_t, scales, None, None)
        mixed_out[:, f] = mixed.T.astype(BF16).reshape(parts, each, width)
        return carry

    lax.fori_loop(0, frames, one_frame, 0, unroll=1)


def mlp_kernel(mixed, after_time, out_w, gain, up, down, block_out, turned):
    count, group, width = mixed.shape
    turned[...] = mixed[...].astype(F32).reshape(count * group, width)

    def one_bin(b, carry):
        mix = turned[pl.ds(b, count, stride=group), :].astype(BF16)
        after_freq = (after_time[b].astype(F32) + dot_nn(mix, out_w[...])).astype(BF16)
        hidden = jax.nn.gelu(dot_nn(layer_norm(after_freq, gain[...]), up[...])).astype(BF16)
        block_out[b] = (after_freq.astype(F32) + dot_nn(hidden, down[...])).astype(BF16)
        return carry

    lax.fori_loop(0, group, one_bin, 0, unroll=2)


def full(array):
    return pl.BlockSpec(array.shape, lambda i: (0,) * array.ndim)


def params():
    return pltpu.CompilerParams(dimension_semantics=("arbitrary",), vmem_limit_bytes=48 << 20)


def time_stage(before, spec, after, bias, eye, time_gain, match, value_t, out_w, freq_gain):
    bins, count, width = spec.shape
    bin_block = lambda n: pl.BlockSpec((GROUP, n, width), lambda i: (i, 0, 0))
    return pl.pallas_call(
        time_kernel,
        grid=(bins // GROUP,),
        in_specs=[bin_block(HALO), bin_block(count), bin_block(HALO)]
        + [full(a) for a in (bias, eye, time_gain, match, value_t, out_w, freq_gain)],
        out_specs=[bin_block(count), pl.BlockSpec((count, GROUP, width), lambda i: (0, i, 0))],
        out_shape=[
            jax.ShapeDtypeStruct((bins, count, width), BF16),
            jax.ShapeDtypeStruct((count, bins, width), BF16),
        ],
        scratch_shapes=[pltpu.VMEM((count * GROUP, width), F32)],
        compiler_params=params(),
        name="time_stage",
    )(before, spec, after, bias, eye, time_gain, match, value_t, out_w, freq_gain)


def freq_stage(rows, match, value_t, step):
    parts, frames, each, width = rows.shape
    block = pl.BlockSpec((parts, step, each, width), lambda i: (0, i, 0, 0))
    return pl.pallas_call(
        freq_kernel,
        grid=(frames // step,),
        in_specs=[block, full(match), full(value_t)],
        out_specs=block,
        out_shape=jax.ShapeDtypeStruct(rows.shape, BF16),
        compiler_params=params(),
        name="freq_stage",
    )(rows, match, value_t)


def mlp_stage(mixed, after_time, out_w, gain, up, down):
    bins, count, width = after_time.shape
    return pl.pallas_call(
        mlp_kernel,
        grid=(bins // GROUP,),
        in_specs=[
            pl.BlockSpec((count, GROUP, width), lambda i: (0, i, 0)),
            pl.BlockSpec((GROUP, count, width), lambda i: (i, 0, 0)),
        ]
        + [full(a) for a in (out_w, gain, up, down)],
        out_specs=pl.BlockSpec((GROUP, count, width), lambda i: (i, 0, 0)),
        out_shape=jax.ShapeDtypeStruct((bins, count, width), BF16),
        scratch_shapes=[pltpu.VMEM((count * GROUP, width), F32)],
        compiler_params=params(),
        name="mlp_stage",
    )(mixed, after_time, out_w, gain, up, down)


def key_bias(segment_ids, active, count):
    frames = segment_ids.shape[0]
    span = count + 2 * HALO
    start = lax.axis_index("tm") * count
    seg_query = lax.dynamic_slice_in_dim(segment_ids, start, count, 0)
    seg_key = lax.dynamic_slice_in_dim(jnp.pad(segment_ids, HALO, constant_values=-1), start, span, 0)
    act_key = lax.dynamic_slice_in_dim(jnp.pad(active, HALO), start, span, 0)
    pos_key = start - HALO + jnp.arange(span, dtype=jnp.int32)
    pos_query = start + jnp.arange(count, dtype=jnp.int32)
    inside = (pos_key >= 0) & (pos_key < frames)
    allowed = (
        inside[:, None]
        & (seg_query[None, :] == seg_key[:, None])
        & ((act_key[:, None] == 1) | (pos_query[None, :] == pos_key[:, None]))
    )
    return jnp.where(allowed, 0.0, NEG).astype(BF16)


def per_device(
    spec,
    segment_ids,
    active,
    time_gain,
    time_match,
    time_value,
    time_out,
    freq_gain,
    freq_match,
    freq_value,
    freq_out,
    mlp_gain,
    mlp_up,
    mlp_down,
):
    bins, count, width = spec.shape
    peers = lax.axis_size("tm")
    split = lax.axis_size("freq")
    up = [(i, i + 1) for i in range(peers - 1)]
    down = [(j, i) for i, j in up]
    before = lax.ppermute(spec[:, count - HALO :], "tm", up)
    after = lax.ppermute(spec[:, :HALO], "tm", down)
    bias = key_bias(segment_ids, active, count)
    after_time, sent = time_stage(
        before,
        spec,
        after,
        bias,
        jnp.eye(count, dtype=BF16),
        time_gain[None],
        time_match,
        time_value.T,
        time_out,
        freq_gain[None],
    )
    gathered = lax.all_to_all(sent, "freq", split_axis=0, concat_axis=0, tiled=True)
    mixed = freq_stage(
        gathered.reshape(split, count // split, bins, width), freq_match, freq_value.T, 4
    )
    returned = lax.all_to_all(
        mixed.reshape(count, bins, width), "freq", split_axis=0, concat_axis=0, tiled=True
    )
    return mlp_stage(returned, after_time, freq_out, mlp_gain[None], mlp_up, mlp_down)


def solution(mesh):
    placed = (P("freq", "tm", None),) + (P(),) * 13
    return jax.shard_map(
        per_device, mesh=mesh, in_specs=placed, out_specs=P("freq", "tm", None), check_vma=False
    )
```

```python
import functools
import math

import jax
import jax.numpy as jnp
from jax import lax
from jax.experimental import pallas as pl
from jax.experimental.pallas import tpu as pltpu
from jax.sharding import PartitionSpec as P

HEADS = 4
HALO = 64
PROJECT_BINS = 4
FINISH_BINS = 4
MLP_BINS = 4
TURN_STEPS = 4
F32 = jnp.float32
BF16 = jnp.bfloat16
NEG = -1e30
ONES_ROWS = 16


def layer_norm(values, gain):
    widened = values.astype(F32)
    centred = widened - jnp.mean(widened, -1, keepdims=True)
    spread = jnp.mean(centred * centred, -1, keepdims=True)
    return (centred * lax.rsqrt(spread + 1e-05) * gain).astype(BF16)


def dot_nt(a, b):
    return lax.dot_general(a, b, (((1,), (1,)), ((), ())), preferred_element_type=F32)


def dot_tn(a, b):
    return lax.dot_general(a, b, (((0,), (0,)), ((), ())), preferred_element_type=F32)


def dot_nn(a, b):
    return jnp.dot(a, b, preferred_element_type=F32)


def head_scales(width):
    head = lax.broadcasted_iota(jnp.int32, (1, width), 1) // (width // HEADS)
    scale = (width // HEADS) ** (-0.5) * math.log2(math.e)
    return [jnp.where(head == h, scale, 0.0).astype(F32) for h in range(HEADS)]


def extended(values_t):
    return jnp.concatenate([values_t, jnp.ones((ONES_ROWS, values_t.shape[1]), BF16)], 0)


def score(key_rows, sides, bias, scores, largest):
    found = dot_nt(key_rows, jnp.concatenate(sides, 0))
    if bias is not None:
        found = found + bias
    scores[...] = found
    largest[...] = jnp.max(found, 0, keepdims=True)


def weigh(scores, largest, weights):
    weights[...] = jnp.exp2(scores[...] - largest[...]).astype(BF16)


def gather(values_t, weights, heads, columns):
    depth = values_t.shape[0] // heads
    pieces = []
    for h in range(heads):
        mixed = dot_nn(extended(values_t[h * depth : (h + 1) * depth]), weights[:, h * columns : (h + 1) * columns])
        pieces.append(mixed[:depth] / mixed[depth : depth + 1])
    return jnp.concatenate(pieces, 0).astype(BF16)


def time_kernel(
    before, own, after, bias, time_gain, match, value_t, out_w, freq_gain,
    after_time, sent, keys, values, mixes, turned, s0, s1, m0, m1, e0, e1,
):
    bins, count, width = own.shape
    span = count + 2 * HALO
    scales = head_scales(width)

    def project(i, carry):
        parts = []
        for j in range(PROJECT_BINS):
            b = i * PROJECT_BINS + j
            parts += [before[b], own[b], after[b]]
        normed = layer_norm(jnp.concatenate(parts, 0), time_gain[...])
        keys[pl.ds(i * PROJECT_BINS, PROJECT_BINS)] = (
            dot_nn(normed, match[...]).astype(BF16).reshape(PROJECT_BINS, span, width)
        )
        found = dot_nt(value_t[...], normed).astype(BF16)
        for j in range(PROJECT_BINS):
            values[i * PROJECT_BINS + j] = found[:, j * span : (j + 1) * span]
        return carry

    lax.fori_loop(0, bins // PROJECT_BINS, project, 0)

    def score_bin(b, scores, largest):
        rows = keys[b]
        wide = rows[HALO : HALO + count].astype(F32)
        sides = [(wide * scale).astype(BF16) for scale in scales]
        score(rows, sides, jnp.concatenate([bias[...]] * HEADS, 1), scores, largest)

    def gather_bin(b, weights):
        mixes[b + 2] = gather(values[jnp.maximum(b, 0)], weights, HEADS, count)

    def attend(i, carry):
        b = jnp.minimum(2 * i, bins - 2)
        score_bin(b, s0, m0)
        weigh(s1, m1, e1)
        gather_bin(2 * i - 2, e0)
        score_bin(b + 1, s1, m1)
        weigh(s0, m0, e0)
        gather_bin(2 * i - 1, e1)
        return carry

    lax.fori_loop(0, bins // 2 + 1, attend, 0)

    def finish(i, carry):
        parts = [dot_tn(mixes[i * FINISH_BINS + j + 2], out_w[...]) for j in range(FINISH_BINS)]
        first = i * FINISH_BINS
        spec = own[pl.ds(first, FINISH_BINS)].astype(F32).reshape(FINISH_BINS * count, width)
        result = (spec + jnp.concatenate(parts, 0)).astype(BF16)
        after_time[pl.ds(first, FINISH_BINS)] = result.reshape(FINISH_BINS, count, width)
        normed = layer_norm(result, freq_gain[...]).astype(F32)
        for j in range(FINISH_BINS):
            turned[pl.ds(first + j, count, stride=bins), :] = normed[j * count : (j + 1) * count]
        return carry

    lax.fori_loop(0, bins // FINISH_BINS, finish, 0)

    def turn(i, carry):
        rows = count // TURN_STEPS
        found = turned[pl.ds(i * rows * bins, rows * bins), :]
        sent[pl.ds(i * rows, rows)] = found.astype(BF16).reshape(rows, bins, width)
        return carry

    lax.fori_loop(0, TURN_STEPS, turn, 0)


def freq_kernel(rows, match, value_t, mixed_out, keys, values, mixes, s0, s1, m0, m1, e0, e1):
    parts, frames, each, width = rows.shape
    bins = parts * each
    scales = head_scales(width)
    half = HEADS // 2

    def project(i, carry):
        normed = jnp.concatenate(
            [rows[:, i * PROJECT_BINS + j].reshape(bins, width) for j in range(PROJECT_BINS)], 0
        )
        keys[pl.ds(i * PROJECT_BINS, PROJECT_BINS)] = (
            dot_nn(normed, match[...]).astype(BF16).reshape(PROJECT_BINS, bins, width)
        )
        found = dot_nt(value_t[...], normed).astype(BF16)
        for j in range(PROJECT_BINS):
            values[i * PROJECT_BINS + j] = found[:, j * bins : (j + 1) * bins]
        return carry

    lax.fori_loop(0, frames // PROJECT_BINS, project, 0)

    def score_pair(f, pair, scores, largest):
        wide = keys[f].astype(F32)
        sides = [(wide * scale).astype(BF16) for scale in scales[pair * half : (pair + 1) * half]]
        score(keys[f], sides, None, scores, largest)

    def gather_pair(f, pair, weights):
        low, high = pair * width // 2, (pair + 1) * width // 2
        mixes[f + 1, low:high] = gather(values[jnp.maximum(f, 0), low:high], weights, half, bins)

    def attend(i, carry):
        f = jnp.minimum(i, frames - 1)
        score_pair(f, 0, s0, m0)
        weigh(s1, m1, e1)
        gather_pair(i - 1, 0, e0)
        score_pair(f, 1, s1, m1)
        weigh(s0, m0, e0)
        gather_pair(i - 1, 1, e1)
        return carry

    lax.fori_loop(0, frames + 1, attend, 0)

    def finish(f, carry):
        mixed_out[:, f] = mixes[f + 1].T.reshape(parts, each, width)
        return carry

    lax.fori_loop(0, frames, finish, 0, unroll=2)


def mlp_kernel(mixed, after_time, out_w, gain, up, down, block_out, turned):
    count, bins, width = mixed.shape

    def turn(i, carry):
        rows = count // TURN_STEPS
        found = mixed[pl.ds(i * rows, rows)].astype(F32).reshape(rows * bins, width)
        turned[pl.ds(i * rows * bins, rows * bins), :] = found
        return carry

    lax.fori_loop(0, TURN_STEPS, turn, 0)

    def some_bins(i, carry):
        first = i * MLP_BINS
        mix = jnp.concatenate(
            [turned[pl.ds(first + j, count, stride=bins), :] for j in range(MLP_BINS)], 0
        ).astype(BF16)
        base = after_time[pl.ds(first, MLP_BINS)].astype(F32).reshape(MLP_BINS * count, width)
        after_freq = (base + dot_nn(mix, out_w[...])).astype(BF16)
        hidden = jax.nn.gelu(dot_nn(layer_norm(after_freq, gain[...]), up[...])).astype(BF16)
        result = (after_freq.astype(F32) + dot_nn(hidden, down[...])).astype(BF16)
        block_out[pl.ds(first, MLP_BINS)] = result.reshape(MLP_BINS, count, width)
        return carry

    lax.fori_loop(0, bins // MLP_BINS, some_bins, 0)


def full(array):
    return pl.BlockSpec(array.shape, lambda i: (0,) * array.ndim)


def params():
    return pltpu.CompilerParams(dimension_semantics=("arbitrary",), vmem_limit_bytes=48 << 20)


def buffers(keys, columns):
    return (
        [pltpu.VMEM((keys, columns), F32)] * 2
        + [pltpu.VMEM((1, columns), F32)] * 2
        + [pltpu.VMEM((keys, columns), BF16)] * 2
    )


def time_stage(before, spec, after, bias, time_gain, match, value_t, out_w, freq_gain):
    bins, count, width = spec.shape
    span = count + 2 * HALO
    args = (before, spec, after, bias, time_gain, match, value_t, out_w, freq_gain)
    shapes = [(bins, count, width), (count, bins, width)]
    return pl.pallas_call(
        time_kernel,
        grid=(1,),
        in_specs=[full(a) for a in args],
        out_specs=[pl.BlockSpec(s, lambda i: (0, 0, 0)) for s in shapes],
        out_shape=[jax.ShapeDtypeStruct(s, BF16) for s in shapes],
        scratch_shapes=[
            pltpu.VMEM((bins, span, width), BF16),
            pltpu.VMEM((bins, width, span), BF16),
            pltpu.VMEM((bins + 2, width, count), BF16),
            pltpu.VMEM((count * bins, width), F32),
        ]
        + buffers(span, HEADS * count),
        compiler_params=params(),
        name="time_stage",
    )(*args)


def freq_stage(rows, match, value_t):
    parts, frames, each, width = rows.shape
    bins = parts * each
    return pl.pallas_call(
        freq_kernel,
        grid=(1,),
        in_specs=[full(rows), full(match), full(value_t)],
        out_specs=full(rows),
        out_shape=jax.ShapeDtypeStruct(rows.shape, BF16),
        scratch_shapes=[
            pltpu.VMEM((frames, bins, width), BF16),
            pltpu.VMEM((frames, width, bins), BF16),
            pltpu.VMEM((frames + 1, width, bins), BF16),
        ]
        + buffers(bins, HEADS // 2 * bins),
        compiler_params=params(),
        name="freq_stage",
    )(rows, match, value_t)


def mlp_stage(mixed, after_time, out_w, gain, up, down):
    bins, count, width = after_time.shape
    args = (mixed, after_time, out_w, gain, up, down)
    return pl.pallas_call(
        mlp_kernel,
        grid=(1,),
        in_specs=[full(a) for a in args],
        out_specs=full(after_time),
        out_shape=jax.ShapeDtypeStruct((bins, count, width), BF16),
        scratch_shapes=[pltpu.VMEM((count * bins, width), F32)],
        compiler_params=params(),
        name="mlp_stage",
    )(*args)


def key_bias(segment_ids, active, count):
    frames = segment_ids.shape[0]
    span = count + 2 * HALO
    start = lax.axis_index("tm") * count
    seg_query = lax.dynamic_slice_in_dim(segment_ids, start, count, 0)
    seg_key = lax.dynamic_slice_in_dim(jnp.pad(segment_ids, HALO, constant_values=-1), start, span, 0)
    act_key = lax.dynamic_slice_in_dim(jnp.pad(active, HALO), start, span, 0)
    pos_key = start - HALO + jnp.arange(span, dtype=jnp.int32)
    pos_query = start + jnp.arange(count, dtype=jnp.int32)
    inside = (pos_key >= 0) & (pos_key < frames)
    allowed = (
        inside[:, None]
        & (seg_query[None, :] == seg_key[:, None])
        & ((act_key[:, None] == 1) | (pos_query[None, :] == pos_key[:, None]))
    )
    return jnp.where(allowed, 0.0, NEG).astype(F32)


def per_device(
    spec,
    segment_ids,
    active,
    time_gain,
    time_match,
    time_value,
    time_out,
    freq_gain,
    freq_match,
    freq_value,
    freq_out,
    mlp_gain,
    mlp_up,
    mlp_down,
):
    bins, count, width = spec.shape
    peers = lax.axis_size("tm")
    split = lax.axis_size("freq")
    up = [(i, i + 1) for i in range(peers - 1)]
    down = [(j, i) for i, j in up]
    before = lax.ppermute(spec[:, count - HALO :], "tm", up)
    after = lax.ppermute(spec[:, :HALO], "tm", down)
    bias = key_bias(segment_ids, active, count)
    after_time, sent = time_stage(
        before,
        spec,
        after,
        bias,
        time_gain[None],
        time_match,
        time_value.T,
        time_out,
        freq_gain[None],
    )
    gathered = lax.all_to_all(sent, "freq", split_axis=0, concat_axis=0, tiled=True)
    mixed = freq_stage(
        gathered.reshape(split, count // split, bins, width), freq_match, freq_value.T
    )
    returned = lax.all_to_all(
        mixed.reshape(count, bins, width), "freq", split_axis=0, concat_axis=0, tiled=True
    )
    return mlp_stage(returned, after_time, freq_out, mlp_gain[None], mlp_up, mlp_down)


def solution(mesh):
    placed = (P("freq", "tm", None),) + (P(),) * 13
    return jax.shard_map(
        per_device, mesh=mesh, in_specs=placed, out_specs=P("freq", "tm", None), check_vma=False
    )
```

```python
import functools
import math

import jax
import jax.numpy as jnp
from jax import lax
from jax.experimental import pallas as pl
from jax.experimental.pallas import tpu as pltpu
from jax.sharding import PartitionSpec as P

HEADS = 4
HALO = 64
CHUNKS = 1
UNIT_BINS = 4
F32 = jnp.float32
BF16 = jnp.bfloat16
NEG = -1e30
ONES_ROWS = 16


def layer_norm(values, gain):
    widened = values.astype(F32)
    centred = widened - jnp.mean(widened, -1, keepdims=True)
    spread = jnp.mean(centred * centred, -1, keepdims=True)
    return (centred * lax.rsqrt(spread + 1e-05) * gain).astype(BF16)


def dot_nt(a, b):
    return lax.dot_general(a, b, (((1,), (1,)), ((), ())), preferred_element_type=F32)


def dot_tn(a, b):
    return lax.dot_general(a, b, (((0,), (0,)), ((), ())), preferred_element_type=F32)


def dot_nn(a, b):
    return jnp.dot(a, b, preferred_element_type=F32)


def query_sides(rows):
    width = rows.shape[1]
    wide = rows.astype(F32)
    head = lax.broadcasted_iota(jnp.int32, (1, width), 1) // (width // HEADS)
    scale = (width // HEADS) ** (-0.5) * math.log2(math.e)
    return jnp.concatenate(
        [(wide * jnp.where(head == h, scale, 0.0).astype(F32)).astype(BF16) for h in range(HEADS)], 0
    )


def head_pairs(values_t, weights):
    depth = values_t.shape[0] // HEADS
    columns = weights.shape[1] // HEADS
    ones = jnp.ones((ONES_ROWS, values_t.shape[1]), BF16)
    for p in range(HEADS // 2):
        low, high = 2 * p * depth, 2 * (p + 1) * depth
        found = dot_nn(
            jnp.concatenate([values_t[low:high], ones], 0), weights[:, 2 * p * columns : 2 * (p + 1) * columns]
        )
        for j in range(2):
            side = slice(j * columns, (j + 1) * columns)
            yield 2 * p + j, found[j * depth : (j + 1) * depth, side], found[2 * depth : 2 * depth + 1, side]


def pipelined(units, stages):
    count = len(stages)

    def run(u, first, last):
        for s in reversed(range(first, last)):
            stages[s](u - s)

    def step(u, carry):
        run(u, 0, count)
        return carry

    for u in range(count - 1):
        run(u, 0, u + 1)
    lax.fori_loop(count - 1, units, step, 0)
    for u in range(units, units + count - 1):
        run(u, u - units + 1, count)


def both(*stages):
    def run(u):
        for stage in stages:
            stage(u)

    return run


def project_rows(joined, match, value_t, keys, values, first, span):
    width = joined.shape[1]
    some = joined.shape[0] // span
    keys[pl.ds(first, some)] = dot_nn(joined, match[...]).astype(BF16).reshape(some, span, width)
    found = dot_nt(value_t[...], joined).astype(BF16)
    for j in range(some):
        values[first + j] = found[:, j * span : (j + 1) * span]


def own_kernel(own, bias, gain, match, value_t, keys, part_mix, part_max, part_sum, values, scores, weights):
    bins, count, width = own.shape
    depth = width // HEADS

    def project(u):
        first = u * UNIT_BINS
        rows = own[pl.ds(first, UNIT_BINS)].reshape(UNIT_BINS * count, width)
        project_rows(layer_norm(rows, gain[...]), match, value_t, keys, values, first, count)

    def score(u):
        for j in range(UNIT_BINS):
            b = u * UNIT_BINS + j
            found = dot_nt(keys[b], query_sides(keys[b])) + jnp.concatenate([bias[...]] * HEADS, 1)
            scores[j] = found
            part_max[b] = jnp.max(found, 0, keepdims=True)

    def weigh(u):
        for j in range(UNIT_BINS):
            weights[j] = jnp.exp2(scores[j] - part_max[u * UNIT_BINS + j]).astype(BF16)

    def gather(u):
        for j in range(UNIT_BINS):
            b = u * UNIT_BINS + j
            for h, mixed, total in head_pairs(values[b], weights[j]):
                part_mix[b, h * depth : (h + 1) * depth] = mixed
                part_sum[b, :, h * count : (h + 1) * count] = total

    pipelined(bins // UNIT_BINS, [project, score, weigh, gather])


def halo_kernel(
    before, own, after, bias, gain, match, value_t, out_w, freq_gain, queries, part_mix, part_max, part_sum,
    after_time, *rest
):
    sent, (keys, values, mixes, turned, scores, weights, largest, faded) = rest[:CHUNKS], rest[CHUNKS:]
    bins, count, width = own.shape
    depth = width // HEADS
    parts = sent[0].shape[0]

    def project(u):
        first = u * UNIT_BINS
        rows = []
        for j in range(UNIT_BINS):
            rows += [before[first + j], after[first + j]]
        normed = layer_norm(jnp.concatenate(rows, 0), gain[...])
        project_rows(normed, match, value_t, keys, values, first, 2 * HALO)

    def score(u):
        for j in range(UNIT_BINS):
            b = u * UNIT_BINS + j
            found = dot_nt(keys[b], query_sides(queries[b])) + jnp.concatenate([bias[...]] * HEADS, 1)
            scores[j] = found
            largest[j] = jnp.maximum(jnp.max(found, 0, keepdims=True), part_max[b])

    def weigh(u):
        for j in range(UNIT_BINS):
            weights[j] = jnp.exp2(scores[j] - largest[j]).astype(BF16)
            faded[j] = jnp.exp2(part_max[u * UNIT_BINS + j] - largest[j])

    def gather(u):
        for j in range(UNIT_BINS):
            b = u * UNIT_BINS + j
            for h, mixed, total in head_pairs(values[b], weights[j]):
                columns = slice(h * count, (h + 1) * count)
                fade = faded[j, :, columns]
                mixed = mixed + part_mix[b, h * depth : (h + 1) * depth] * fade
                total = total + part_sum[b, :, columns] * fade
                mixes[j, h * depth : (h + 1) * depth] = (mixed * (1.0 / total)).astype(BF16)

    def finish(u):
        first = u * UNIT_BINS
        found = [dot_tn(mixes[j], out_w[...]) for j in range(UNIT_BINS)]
        spec = own[pl.ds(first, UNIT_BINS)].astype(F32).reshape(UNIT_BINS * count, width)
        result = (spec + jnp.concatenate(found, 0)).astype(BF16)
        after_time[pl.ds(first, UNIT_BINS)] = result.reshape(UNIT_BINS, count, width)
        normed = layer_norm(result, freq_gain[...]).astype(F32)
        for j in range(UNIT_BINS):
            turned[pl.ds(first + j, count, stride=bins), :] = normed[j * count : (j + 1) * count]

    pipelined(bins // UNIT_BINS, [project, score, both(weigh, gather), finish])
    each = count // parts // CHUNKS

    def turn(d, carry):
        for c in range(CHUNKS):
            found = turned[pl.ds((c * parts + d) * each * bins, each * bins), :]
            sent[c][d] = found.astype(BF16).reshape(each, bins, width)
        return carry

    lax.fori_loop(0, parts, turn, 0)


def freq_kernel(rows, match, value_t, mixed_out, keys, values, scores, weights, largest):
    parts, frames, each, width = rows.shape
    bins = parts * each
    depth = width // HEADS

    def project(f):
        project_rows(rows[:, f].reshape(bins, width), match, value_t, keys, values, f, bins)

    def score(f):
        found = dot_nt(query_sides(keys[f]), keys[f])
        scores[...] = found
        for h in range(HEADS):
            largest[h : h + 1] = jnp.max(found[h * bins : (h + 1) * bins], 0, keepdims=True)

    def weigh(f):
        for h in range(HEADS):
            part = slice(h * bins, (h + 1) * bins)
            weights[part] = jnp.exp2(scores[part] - largest[h : h + 1]).astype(BF16)

    def gather(f):
        pieces = []
        ones = jnp.ones((ONES_ROWS, bins), BF16)
        for h in range(HEADS):
            own = jnp.concatenate([values[f, h * depth : (h + 1) * depth], ones], 0)
            found = dot_nn(own, weights[h * bins : (h + 1) * bins])
            pieces.append(found[:depth] * (1.0 / found[depth : depth + 1]))
        mixed_out[:, f] = jnp.concatenate(pieces, 0).T.astype(BF16).reshape(parts, each, width)

    pipelined(frames, [project, score, weigh, gather])


def full(array):
    return pl.BlockSpec(array.shape, lambda i: (0,) * len(array.shape))


def block(shape, *index):
    return pl.BlockSpec(shape, lambda i: index)


def call(kernel, name, us, **kwargs):
    return pl.pallas_call(
        kernel,
        grid=(1,),
        compiler_params=pltpu.CompilerParams(
            dimension_semantics=("arbitrary",), vmem_limit_bytes=14 << 20
        ),
        cost_estimate=pl.CostEstimate(flops=int(us * 5e8), bytes_accessed=1 << 20, transcendentals=0),
        name=name,
        **kwargs,
    )


def own_stage(spec, bias, gain, match, value_t):
    bins, count, width = spec.shape
    columns = HEADS * count
    args = (spec, bias, gain, match, value_t)
    outs = [
        jax.ShapeDtypeStruct((bins, count, width), BF16),
        jax.ShapeDtypeStruct((bins, width, count), F32),
        jax.ShapeDtypeStruct((bins, 1, columns), F32),
        jax.ShapeDtypeStruct((bins, 1, columns), F32),
    ]
    return call(
        own_kernel,
        "own_stage",
        8,
        in_specs=[full(a) for a in args],
        out_specs=[full(o) for o in outs],
        out_shape=outs,
        scratch_shapes=[
            pltpu.VMEM((bins, width, count), BF16),
            pltpu.VMEM((UNIT_BINS, count, columns), F32),
            pltpu.VMEM((UNIT_BINS, count, columns), BF16),
        ],
    )(*args)


def halo_stage(parts, before, spec, after, bias, gain, match, value_t, out_w, freq_gain, partial):
    bins, count, width = spec.shape
    columns = HEADS * count
    args = (before, spec, after, bias, gain, match, value_t, out_w, freq_gain, *partial)
    outs = [jax.ShapeDtypeStruct((bins, count, width), BF16)] + [
        jax.ShapeDtypeStruct((parts, count // parts // CHUNKS, bins, width), BF16)
    ] * CHUNKS
    return call(
        halo_kernel,
        "halo_stage",
        7,
        in_specs=[full(a) for a in args],
        out_specs=[full(o) for o in outs],
        out_shape=outs,
        scratch_shapes=[
            pltpu.VMEM((bins, 2 * HALO, width), BF16),
            pltpu.VMEM((bins, width, 2 * HALO), BF16),
            pltpu.VMEM((UNIT_BINS, width, count), BF16),
            pltpu.VMEM((count * bins, width), F32),
            pltpu.VMEM((UNIT_BINS, 2 * HALO, columns), F32),
            pltpu.VMEM((UNIT_BINS, 2 * HALO, columns), BF16),
            pltpu.VMEM((UNIT_BINS, 1, columns), F32),
            pltpu.VMEM((UNIT_BINS, 1, columns), F32),
        ],
    )(*args)


def freq_stage(rows, match, value_t):
    parts, frames, each, width = rows.shape
    bins = parts * each
    return call(
        freq_kernel,
        "freq_stage",
        5,
        in_specs=[full(rows), full(match), full(value_t)],
        out_specs=full(rows),
        out_shape=jax.ShapeDtypeStruct(rows.shape, BF16),
        scratch_shapes=[
            pltpu.VMEM((frames, bins, width), BF16),
            pltpu.VMEM((frames, width, bins), BF16),
            pltpu.VMEM((HEADS * bins, bins), F32),
            pltpu.VMEM((HEADS * bins, bins), BF16),
            pltpu.VMEM((HEADS, bins), F32),
        ],
    )(rows, match, value_t)


def add_branch(base, mixed, weight):
    return (base.astype(F32) + dot_nn(mixed, weight)).astype(BF16)


def feed_forward(after_freq, mlp_gain, mlp_up, mlp_down):
    hidden = jax.nn.gelu(dot_nn(layer_norm(after_freq, mlp_gain), mlp_up)).astype(BF16)
    return add_branch(after_freq, hidden, mlp_down)


def key_bias(segment_ids, active, count):
    frames = segment_ids.shape[0]
    span = count + 2 * HALO
    start = lax.axis_index("tm") * count
    seg_query = lax.dynamic_slice_in_dim(segment_ids, start, count, 0)
    seg_key = lax.dynamic_slice_in_dim(jnp.pad(segment_ids, HALO, constant_values=-1), start, span, 0)
    act_key = lax.dynamic_slice_in_dim(jnp.pad(active, HALO), start, span, 0)
    pos_key = start - HALO + jnp.arange(span, dtype=jnp.int32)
    pos_query = start + jnp.arange(count, dtype=jnp.int32)
    inside = (pos_key >= 0) & (pos_key < frames)
    allowed = (
        inside[:, None]
        & (seg_query[None, :] == seg_key[:, None])
        & ((act_key[:, None] == 1) | (pos_query[None, :] == pos_key[:, None]))
    )
    return jnp.where(allowed, 0.0, NEG).astype(F32)


def per_device(
    spec,
    segment_ids,
    active,
    time_gain,
    time_match,
    time_value,
    time_out,
    freq_gain,
    freq_match,
    freq_value,
    freq_out,
    mlp_gain,
    mlp_up,
    mlp_down,
):
    bins, count, width = spec.shape
    peers = lax.axis_size("tm")
    parts = lax.axis_size("freq")
    up = [(i, i + 1) for i in range(peers - 1)]
    down = [(j, i) for i, j in up]
    before = lax.ppermute(spec[:, count - HALO :], "tm", up)
    after = lax.ppermute(spec[:, :HALO], "tm", down)
    bias = key_bias(segment_ids, active, count)
    side_bias = jnp.concatenate([bias[:HALO], bias[HALO + count :]], 0)
    time_value_t, freq_value_t = time_value.T, freq_value.T
    partial = own_stage(spec, bias[HALO : HALO + count], time_gain[None], time_match, time_value_t)
    base, *sent = halo_stage(
        parts, before, spec, after, side_bias, time_gain[None], time_match, time_value_t, time_out, freq_gain[None],
        partial,
    )
    base, *sent = lax.optimization_barrier((jnp.swapaxes(base, 0, 1), *sent))
    gathered = [exchange(s) for s in sent]
    returned = [exchange(freq_stage(g, freq_match, freq_value_t)) for g in gathered]
    mixed = returned[0].reshape(count, bins, width)
    after_freq = add_branch(base, mixed, freq_out)
    result = lax.optimization_barrier(feed_forward(after_freq, mlp_gain, mlp_up, mlp_down))
    return jnp.swapaxes(result, 0, 1)


def exchange(array):
    return lax.all_to_all(array, "freq", split_axis=0, concat_axis=0, tiled=True)


def solution(mesh):
    placed = (P("freq", "tm", None),) + (P(),) * 13
    return jax.shard_map(
        per_device, mesh=mesh, in_specs=placed, out_specs=P("freq", "tm", None), check_vma=False
    )
```

```python
import functools
import math

import jax
import jax.numpy as jnp
from jax import lax
from jax.experimental import pallas as pl
from jax.experimental.pallas import tpu as pltpu
from jax.sharding import PartitionSpec as P

HEADS = 4
HALO = 64
CHUNKS = 1
UNIT_BINS = 4
F32 = jnp.float32
BF16 = jnp.bfloat16
NEG = -1e30
ONES_ROWS = 16


def layer_norm(values, gain):
    widened = values.astype(F32)
    centred = widened - jnp.mean(widened, -1, keepdims=True)
    spread = jnp.mean(centred * centred, -1, keepdims=True)
    return (centred * lax.rsqrt(spread + 1e-05) * gain).astype(BF16)


def dot_nt(a, b):
    return lax.dot_general(a, b, (((1,), (1,)), ((), ())), preferred_element_type=F32)


def dot_tn(a, b):
    return lax.dot_general(a, b, (((0,), (0,)), ((), ())), preferred_element_type=F32)


def dot_nn(a, b):
    return jnp.dot(a, b, preferred_element_type=F32)


def query_sides(rows):
    width = rows.shape[1]
    wide = rows.astype(F32)
    head = lax.broadcasted_iota(jnp.int32, (1, width), 1) // (width // HEADS)
    scale = (width // HEADS) ** (-0.5) * math.log2(math.e)
    return jnp.concatenate(
        [(wide * jnp.where(head == h, scale, 0.0).astype(F32)).astype(BF16) for h in range(HEADS)], 0
    )


def head_pairs(values_t, weights):
    depth = values_t.shape[0] // HEADS
    columns = weights.shape[1] // HEADS
    ones = jnp.ones((ONES_ROWS, values_t.shape[1]), BF16)
    for p in range(HEADS // 2):
        low, high = 2 * p * depth, 2 * (p + 1) * depth
        found = dot_nn(
            jnp.concatenate([values_t[low:high], ones], 0), weights[:, 2 * p * columns : 2 * (p + 1) * columns]
        )
        for j in range(2):
            side = slice(j * columns, (j + 1) * columns)
            yield 2 * p + j, found[j * depth : (j + 1) * depth, side], found[2 * depth : 2 * depth + 1, side]


def pipelined(units, stages):
    count = len(stages)

    def run(u, first, last):
        for s in reversed(range(first, last)):
            stages[s](u - s)

    def step(u, carry):
        run(u, 0, count)
        return carry

    for u in range(count - 1):
        run(u, 0, u + 1)
    lax.fori_loop(count - 1, units, step, 0)
    for u in range(units, units + count - 1):
        run(u, u - units + 1, count)


def both(*stages):
    def run(u):
        for stage in stages:
            stage(u)

    return run


def project_rows(joined, match, value_t, keys, values, first, span):
    width = joined.shape[1]
    some = joined.shape[0] // span
    keys[pl.ds(first, some)] = dot_nn(joined, match[...]).astype(BF16).reshape(some, span, width)
    found = dot_nt(value_t[...], joined).astype(BF16)
    for j in range(some):
        values[first + j] = found[:, j * span : (j + 1) * span]


def own_kernel(own, bias, gain, match, value_t, keys, part_mix, part_max, part_sum, values, scores, weights):
    bins, count, width = own.shape
    depth = width // HEADS

    def project(u):
        first = u * UNIT_BINS
        rows = own[pl.ds(first, UNIT_BINS)].reshape(UNIT_BINS * count, width)
        project_rows(layer_norm(rows, gain[...]), match, value_t, keys, values, first, count)

    def score(u):
        for j in range(UNIT_BINS):
            b = u * UNIT_BINS + j
            found = dot_nt(keys[b], query_sides(keys[b])) + jnp.concatenate([bias[...]] * HEADS, 1)
            scores[j] = found
            part_max[b] = jnp.max(found, 0, keepdims=True)

    def weigh(u):
        for j in range(UNIT_BINS):
            weights[j] = jnp.exp2(scores[j] - part_max[u * UNIT_BINS + j]).astype(BF16)

    def gather(u):
        for j in range(UNIT_BINS):
            b = u * UNIT_BINS + j
            for h, mixed, total in head_pairs(values[b], weights[j]):
                part_mix[b, h * depth : (h + 1) * depth] = mixed
                part_sum[b, :, h * count : (h + 1) * count] = total

    pipelined(bins // UNIT_BINS, [project, score, weigh, gather])


def halo_kernel(
    before, own, after, bias, gain, match, value_t, out_w, freq_gain, queries, part_mix, part_max, part_sum,
    after_time, *rest
):
    sent, (keys, values, mixes, turned, scores, weights, largest, faded) = rest[:CHUNKS], rest[CHUNKS:]
    bins, count, width = own.shape
    depth = width // HEADS
    parts = sent[0].shape[0]

    def project(u):
        first = u * UNIT_BINS
        rows = []
        for j in range(UNIT_BINS):
            rows += [before[first + j], after[first + j]]
        normed = layer_norm(jnp.concatenate(rows, 0), gain[...])
        project_rows(normed, match, value_t, keys, values, first, 2 * HALO)

    def score(u):
        for j in range(UNIT_BINS):
            b = u * UNIT_BINS + j
            found = dot_nt(keys[b], query_sides(queries[b])) + jnp.concatenate([bias[...]] * HEADS, 1)
            scores[j] = found
            largest[j] = jnp.maximum(jnp.max(found, 0, keepdims=True), part_max[b])

    def weigh(u):
        for j in range(UNIT_BINS):
            weights[j] = jnp.exp2(scores[j] - largest[j]).astype(BF16)
            faded[j] = jnp.exp2(part_max[u * UNIT_BINS + j] - largest[j])

    def gather(u):
        for j in range(UNIT_BINS):
            b = u * UNIT_BINS + j
            for h, mixed, total in head_pairs(values[b], weights[j]):
                columns = slice(h * count, (h + 1) * count)
                fade = faded[j, :, columns]
                mixed = mixed + part_mix[b, h * depth : (h + 1) * depth] * fade
                total = total + part_sum[b, :, columns] * fade
                mixes[j, h * depth : (h + 1) * depth] = (mixed * (1.0 / total)).astype(BF16)

    def finish(u):
        first = u * UNIT_BINS
        found = [dot_tn(mixes[j], out_w[...]) for j in range(UNIT_BINS)]
        spec = own[pl.ds(first, UNIT_BINS)].astype(F32).reshape(UNIT_BINS * count, width)
        result = (spec + jnp.concatenate(found, 0)).astype(BF16)
        after_time[pl.ds(first, UNIT_BINS)] = result.reshape(UNIT_BINS, count, width)
        normed = layer_norm(result, freq_gain[...]).astype(F32)
        for j in range(UNIT_BINS):
            turned[pl.ds(first + j, count, stride=bins), :] = normed[j * count : (j + 1) * count]

    pipelined(bins // UNIT_BINS, [project, score, both(weigh, gather), finish])
    each = count // parts // CHUNKS

    def turn(d, carry):
        for c in range(CHUNKS):
            found = turned[pl.ds((c * parts + d) * each * bins, each * bins), :]
            sent[c][d] = found.astype(BF16).reshape(each, bins, width)
        return carry

    lax.fori_loop(0, parts, turn, 0)


def freq_kernel(rows, match, value_t, mixed_out, keys, values, scores, weights, largest):
    parts, frames, each, width = rows.shape
    bins = parts * each
    depth = width // HEADS

    def project(f):
        project_rows(rows[:, f].reshape(bins, width), match, value_t, keys, values, f, bins)

    def score(f):
        found = dot_nt(query_sides(keys[f]), keys[f])
        scores[...] = found
        for h in range(HEADS):
            largest[h : h + 1] = jnp.max(found[h * bins : (h + 1) * bins], 0, keepdims=True)

    def weigh(f):
        for h in range(HEADS):
            part = slice(h * bins, (h + 1) * bins)
            weights[part] = jnp.exp2(scores[part] - largest[h : h + 1]).astype(BF16)

    def gather(f):
        pieces = []
        ones = jnp.ones((ONES_ROWS, bins), BF16)
        for h in range(HEADS):
            own = jnp.concatenate([values[f, h * depth : (h + 1) * depth], ones], 0)
            found = dot_nn(own, weights[h * bins : (h + 1) * bins])
            pieces.append(found[:depth] * (1.0 / found[depth : depth + 1]))
        mixed_out[:, f] = jnp.concatenate(pieces, 0).T.astype(BF16).reshape(parts, each, width)

    pipelined(frames, [project, score, weigh, gather])


def full(array):
    return pl.BlockSpec(array.shape, lambda i: (0,) * len(array.shape))


def block(shape, *index):
    return pl.BlockSpec(shape, lambda i: index)


def call(kernel, name, us, **kwargs):
    return pl.pallas_call(
        kernel,
        grid=(1,),
        compiler_params=pltpu.CompilerParams(
            dimension_semantics=("arbitrary",), vmem_limit_bytes=8 << 20
        ),
        cost_estimate=pl.CostEstimate(flops=int(us * 5e8), bytes_accessed=1 << 20, transcendentals=0),
        name=name,
        **kwargs,
    )


def own_stage(spec, bias, gain, match, value_t):
    bins, count, width = spec.shape
    columns = HEADS * count
    args = (spec, bias, gain, match, value_t)
    outs = [
        jax.ShapeDtypeStruct((bins, count, width), BF16),
        jax.ShapeDtypeStruct((bins, width, count), F32),
        jax.ShapeDtypeStruct((bins, 1, columns), F32),
        jax.ShapeDtypeStruct((bins, 1, columns), F32),
    ]
    return call(
        own_kernel,
        "own_stage",
        8,
        in_specs=[full(a) for a in args],
        out_specs=[full(o) for o in outs],
        out_shape=outs,
        scratch_shapes=[
            pltpu.VMEM((bins, width, count), BF16),
            pltpu.VMEM((UNIT_BINS, count, columns), F32),
            pltpu.VMEM((UNIT_BINS, count, columns), BF16),
        ],
    )(*args)


def halo_stage(parts, before, spec, after, bias, gain, match, value_t, out_w, freq_gain, partial):
    bins, count, width = spec.shape
    columns = HEADS * count
    args = (before, spec, after, bias, gain, match, value_t, out_w, freq_gain, *partial)
    outs = [jax.ShapeDtypeStruct((bins, count, width), BF16)] + [
        jax.ShapeDtypeStruct((parts, count // parts // CHUNKS, bins, width), BF16)
    ] * CHUNKS
    return call(
        halo_kernel,
        "halo_stage",
        7,
        in_specs=[full(a) for a in args],
        out_specs=[full(o) for o in outs],
        out_shape=outs,
        scratch_shapes=[
            pltpu.VMEM((bins, 2 * HALO, width), BF16),
            pltpu.VMEM((bins, width, 2 * HALO), BF16),
            pltpu.VMEM((UNIT_BINS, width, count), BF16),
            pltpu.VMEM((count * bins, width), F32),
            pltpu.VMEM((UNIT_BINS, 2 * HALO, columns), F32),
            pltpu.VMEM((UNIT_BINS, 2 * HALO, columns), BF16),
            pltpu.VMEM((UNIT_BINS, 1, columns), F32),
            pltpu.VMEM((UNIT_BINS, 1, columns), F32),
        ],
    )(*args)


def freq_stage(rows, match, value_t):
    parts, frames, each, width = rows.shape
    bins = parts * each
    return call(
        freq_kernel,
        "freq_stage",
        5,
        in_specs=[full(rows), full(match), full(value_t)],
        out_specs=full(rows),
        out_shape=jax.ShapeDtypeStruct(rows.shape, BF16),
        scratch_shapes=[
            pltpu.VMEM((frames, bins, width), BF16),
            pltpu.VMEM((frames, width, bins), BF16),
            pltpu.VMEM((HEADS * bins, bins), F32),
            pltpu.VMEM((HEADS * bins, bins), BF16),
            pltpu.VMEM((HEADS, bins), F32),
        ],
    )(rows, match, value_t)


def add_branch(base, mixed, weight):
    return (base.astype(F32) + dot_nn(mixed, weight)).astype(BF16)


def feed_forward(after_freq, mlp_gain, mlp_up, mlp_down):
    hidden = jax.nn.gelu(dot_nn(layer_norm(after_freq, mlp_gain), mlp_up)).astype(BF16)
    return add_branch(after_freq, hidden, mlp_down)


def key_bias(segment_ids, active, count):
    frames = segment_ids.shape[0]
    span = count + 2 * HALO
    start = lax.axis_index("tm") * count
    seg_query = lax.dynamic_slice_in_dim(segment_ids, start, count, 0)
    seg_key = lax.dynamic_slice_in_dim(jnp.pad(segment_ids, HALO, constant_values=-1), start, span, 0)
    act_key = lax.dynamic_slice_in_dim(jnp.pad(active, HALO), start, span, 0)
    pos_key = start - HALO + jnp.arange(span, dtype=jnp.int32)
    pos_query = start + jnp.arange(count, dtype=jnp.int32)
    inside = (pos_key >= 0) & (pos_key < frames)
    allowed = (
        inside[:, None]
        & (seg_query[None, :] == seg_key[:, None])
        & ((act_key[:, None] == 1) | (pos_query[None, :] == pos_key[:, None]))
    )
    return jnp.where(allowed, 0.0, NEG).astype(F32)


def per_device(
    spec,
    segment_ids,
    active,
    time_gain,
    time_match,
    time_value,
    time_out,
    freq_gain,
    freq_match,
    freq_value,
    freq_out,
    mlp_gain,
    mlp_up,
    mlp_down,
):
    bins, count, width = spec.shape
    peers = lax.axis_size("tm")
    parts = lax.axis_size("freq")
    up = [(i, i + 1) for i in range(peers - 1)]
    down = [(j, i) for i, j in up]
    before = lax.ppermute(spec[:, count - HALO :], "tm", up)
    after = lax.ppermute(spec[:, :HALO], "tm", down)
    bias = key_bias(segment_ids, active, count)
    side_bias = jnp.concatenate([bias[:HALO], bias[HALO + count :]], 0)
    time_value_t, freq_value_t = time_value.T, freq_value.T
    partial = own_stage(spec, bias[HALO : HALO + count], time_gain[None], time_match, time_value_t)
    base, *sent = halo_stage(
        parts, before, spec, after, side_bias, time_gain[None], time_match, time_value_t, time_out, freq_gain[None],
        partial,
    )
    base, freq_value_t, *sent = lax.optimization_barrier((jnp.swapaxes(base, 0, 1), freq_value_t, *sent))
    gathered = [exchange(s) for s in sent]
    returned = [exchange(freq_stage(g, freq_match, freq_value_t)) for g in gathered]
    mixed = returned[0].reshape(count, bins, width)
    after_freq = add_branch(base, mixed, freq_out)
    result = lax.optimization_barrier(feed_forward(after_freq, mlp_gain, mlp_up, mlp_down))
    return jnp.swapaxes(result, 0, 1)


def exchange(array):
    return lax.all_to_all(array, "freq", split_axis=0, concat_axis=0, tiled=True)


def solution(mesh):
    placed = (P("freq", "tm", None),) + (P(),) * 13
    return jax.shard_map(
        per_device, mesh=mesh, in_specs=placed, out_specs=P("freq", "tm", None), check_vma=False
    )
```

```python
import functools
import math

import jax
import jax.numpy as jnp
from jax import lax
from jax.experimental import pallas as pl
from jax.experimental.pallas import tpu as pltpu
from jax.sharding import PartitionSpec as P

HEADS = 4
HALO = 64
CHUNKS = 1
UNIT_BINS = 4
F32 = jnp.float32
BF16 = jnp.bfloat16
NEG = -1e30
ONES_ROWS = 16


def layer_norm(values, gain):
    widened = values.astype(F32)
    centred = widened - jnp.mean(widened, -1, keepdims=True)
    spread = jnp.mean(centred * centred, -1, keepdims=True)
    return (centred * lax.rsqrt(spread + 1e-05) * gain).astype(BF16)


def dot_nt(a, b):
    return lax.dot_general(a, b, (((1,), (1,)), ((), ())), preferred_element_type=F32)


def dot_tn(a, b):
    return lax.dot_general(a, b, (((0,), (0,)), ((), ())), preferred_element_type=F32)


def dot_nn(a, b):
    return jnp.dot(a, b, preferred_element_type=F32)


def query_sides(rows):
    width = rows.shape[1]
    wide = rows.astype(F32)
    head = lax.broadcasted_iota(jnp.int32, (1, width), 1) // (width // HEADS)
    scale = (width // HEADS) ** (-0.5) * math.log2(math.e)
    return jnp.concatenate(
        [(wide * jnp.where(head == h, scale, 0.0).astype(F32)).astype(BF16) for h in range(HEADS)], 0
    )


def head_pairs(values_t, weights):
    depth = values_t.shape[0] // HEADS
    columns = weights.shape[1] // HEADS
    ones = jnp.ones((ONES_ROWS, values_t.shape[1]), BF16)
    for p in range(HEADS // 2):
        low, high = 2 * p * depth, 2 * (p + 1) * depth
        found = dot_nn(
            jnp.concatenate([values_t[low:high], ones], 0), weights[:, 2 * p * columns : 2 * (p + 1) * columns]
        )
        for j in range(2):
            side = slice(j * columns, (j + 1) * columns)
            yield 2 * p + j, found[j * depth : (j + 1) * depth, side], found[2 * depth : 2 * depth + 1, side]


def pipelined(units, stages):
    count = len(stages)

    def run(u, first, last):
        for s in reversed(range(first, last)):
            stages[s](u - s)

    def step(u, carry):
        run(u, 0, count)
        return carry

    for u in range(count - 1):
        run(u, 0, u + 1)
    lax.fori_loop(count - 1, units, step, 0)
    for u in range(units, units + count - 1):
        run(u, u - units + 1, count)


def both(*stages):
    def run(u):
        for stage in stages:
            stage(u)

    return run


def project_rows(joined, match, value_t, keys, values, first, span):
    width = joined.shape[1]
    some = joined.shape[0] // span
    keys[pl.ds(first, some)] = dot_nn(joined, match[...]).astype(BF16).reshape(some, span, width)
    found = dot_nt(value_t[...], joined).astype(BF16)
    for j in range(some):
        values[first + j] = found[:, j * span : (j + 1) * span]


def own_kernel(own, bias, gain, match, value_t, sides, part_mix, part_max, part_sum, keys, values, scores, weights):
    bins, count, width = own.shape
    depth = width // HEADS

    def project(u):
        first = u * UNIT_BINS
        rows = own[pl.ds(first, UNIT_BINS)].reshape(UNIT_BINS * count, width)
        project_rows(layer_norm(rows, gain[...]), match, value_t, keys, values, first, count)

    def score(u):
        for j in range(UNIT_BINS):
            b = u * UNIT_BINS + j
            side = query_sides(keys[b])
            sides[b] = side
            found = dot_nt(keys[b], side) + jnp.concatenate([bias[...]] * HEADS, 1)
            scores[j] = found
            part_max[b] = jnp.max(found, 0, keepdims=True)

    def weigh(u):
        for j in range(UNIT_BINS):
            weights[j] = jnp.exp2(scores[j] - part_max[u * UNIT_BINS + j]).astype(BF16)

    def gather(u):
        for j in range(UNIT_BINS):
            b = u * UNIT_BINS + j
            for h, mixed, total in head_pairs(values[b], weights[j]):
                part_mix[b, h * depth : (h + 1) * depth] = mixed
                part_sum[b, :, h * count : (h + 1) * count] = total

    pipelined(bins // UNIT_BINS, [project, score, weigh, gather])


def halo_kernel(
    before, own, after, bias, gain, match, value_t, out_w, freq_gain, queries, part_mix, part_max, part_sum,
    after_time, *rest
):
    sent, (keys, values, mixes, turned, scores, weights, largest, faded) = rest[:CHUNKS], rest[CHUNKS:]
    bins, count, width = own.shape
    depth = width // HEADS
    parts = sent[0].shape[0]

    def project(u):
        first = u * UNIT_BINS
        rows = []
        for j in range(UNIT_BINS):
            rows += [before[first + j], after[first + j]]
        normed = layer_norm(jnp.concatenate(rows, 0), gain[...])
        project_rows(normed, match, value_t, keys, values, first, 2 * HALO)

    def score(u):
        for j in range(UNIT_BINS):
            b = u * UNIT_BINS + j
            found = dot_nt(keys[b], queries[b]) + jnp.concatenate([bias[...]] * HEADS, 1)
            scores[j] = found
            largest[j] = jnp.maximum(jnp.max(found, 0, keepdims=True), part_max[b])

    def weigh(u):
        for j in range(UNIT_BINS):
            weights[j] = jnp.exp2(scores[j] - largest[j]).astype(BF16)
            faded[j] = jnp.exp2(part_max[u * UNIT_BINS + j] - largest[j])

    def gather(u):
        for j in range(UNIT_BINS):
            b = u * UNIT_BINS + j
            for h, mixed, total in head_pairs(values[b], weights[j]):
                columns = slice(h * count, (h + 1) * count)
                fade = faded[j, :, columns]
                mixed = mixed + part_mix[b, h * depth : (h + 1) * depth] * fade
                total = total + part_sum[b, :, columns] * fade
                mixes[j, h * depth : (h + 1) * depth] = (mixed * (1.0 / total)).astype(BF16)

    def finish(u):
        first = u * UNIT_BINS
        found = [dot_tn(mixes[j], out_w[...]) for j in range(UNIT_BINS)]
        spec = own[pl.ds(first, UNIT_BINS)].astype(F32).reshape(UNIT_BINS * count, width)
        result = (spec + jnp.concatenate(found, 0)).astype(BF16)
        after_time[pl.ds(first, UNIT_BINS)] = result.reshape(UNIT_BINS, count, width)
        normed = layer_norm(result, freq_gain[...]).astype(F32)
        for j in range(UNIT_BINS):
            turned[pl.ds(first + j, count, stride=bins), :] = normed[j * count : (j + 1) * count]

    pipelined(bins // UNIT_BINS, [project, score, both(weigh, gather), finish])
    each = count // parts // CHUNKS

    def turn(d, carry):
        for c in range(CHUNKS):
            found = turned[pl.ds((c * parts + d) * each * bins, each * bins), :]
            sent[c][d] = found.astype(BF16).reshape(each, bins, width)
        return carry

    lax.fori_loop(0, parts, turn, 0)


def freq_kernel(rows, match, value_t, mixed_out, keys, values, scores, weights, largest):
    parts, frames, each, width = rows.shape
    bins = parts * each
    depth = width // HEADS

    def project(f):
        project_rows(rows[:, f].reshape(bins, width), match, value_t, keys, values, f, bins)

    def score(f):
        found = dot_nt(query_sides(keys[f]), keys[f])
        scores[...] = found
        for h in range(HEADS):
            largest[h : h + 1] = jnp.max(found[h * bins : (h + 1) * bins], 0, keepdims=True)

    def weigh(f):
        for h in range(HEADS):
            part = slice(h * bins, (h + 1) * bins)
            weights[part] = jnp.exp2(scores[part] - largest[h : h + 1]).astype(BF16)

    def gather(f):
        pieces = []
        ones = jnp.ones((ONES_ROWS, bins), BF16)
        for h in range(HEADS):
            own = jnp.concatenate([values[f, h * depth : (h + 1) * depth], ones], 0)
            found = dot_nn(own, weights[h * bins : (h + 1) * bins])
            pieces.append(found[:depth] * (1.0 / found[depth : depth + 1]))
        mixed_out[:, f] = jnp.concatenate(pieces, 0).T.astype(BF16).reshape(parts, each, width)

    pipelined(frames, [project, score, weigh, gather])


def full(array):
    return pl.BlockSpec(array.shape, lambda i: (0,) * len(array.shape))


def block(shape, *index):
    return pl.BlockSpec(shape, lambda i: index)


def call(kernel, name, us, **kwargs):
    return pl.pallas_call(
        kernel,
        grid=(1,),
        compiler_params=pltpu.CompilerParams(
            dimension_semantics=("arbitrary",), vmem_limit_bytes=8 << 20
        ),
        cost_estimate=pl.CostEstimate(flops=int(us * 5e8), bytes_accessed=1 << 20, transcendentals=0),
        name=name,
        **kwargs,
    )


def own_stage(spec, bias, gain, match, value_t):
    bins, count, width = spec.shape
    columns = HEADS * count
    args = (spec, bias, gain, match, value_t)
    outs = [
        jax.ShapeDtypeStruct((bins, columns, width), BF16),
        jax.ShapeDtypeStruct((bins, width, count), F32),
        jax.ShapeDtypeStruct((bins, 1, columns), F32),
        jax.ShapeDtypeStruct((bins, 1, columns), F32),
    ]
    return call(
        own_kernel,
        "own_stage",
        8,
        in_specs=[full(a) for a in args],
        out_specs=[full(o) for o in outs],
        out_shape=outs,
        scratch_shapes=[
            pltpu.VMEM((bins, count, width), BF16),
            pltpu.VMEM((bins, width, count), BF16),
            pltpu.VMEM((UNIT_BINS, count, columns), F32),
            pltpu.VMEM((UNIT_BINS, count, columns), BF16),
        ],
    )(*args)


def halo_stage(parts, before, spec, after, bias, gain, match, value_t, out_w, freq_gain, partial):
    bins, count, width = spec.shape
    columns = HEADS * count
    args = (before, spec, after, bias, gain, match, value_t, out_w, freq_gain, *partial)
    outs = [jax.ShapeDtypeStruct((bins, count, width), BF16)] + [
        jax.ShapeDtypeStruct((parts, count // parts // CHUNKS, bins, width), BF16)
    ] * CHUNKS
    return call(
        halo_kernel,
        "halo_stage",
        7,
        in_specs=[full(a) for a in args],
        out_specs=[full(o) for o in outs],
        out_shape=outs,
        scratch_shapes=[
            pltpu.VMEM((bins, 2 * HALO, width), BF16),
            pltpu.VMEM((bins, width, 2 * HALO), BF16),
            pltpu.VMEM((UNIT_BINS, width, count), BF16),
            pltpu.VMEM((count * bins, width), F32),
            pltpu.VMEM((UNIT_BINS, 2 * HALO, columns), F32),
            pltpu.VMEM((UNIT_BINS, 2 * HALO, columns), BF16),
            pltpu.VMEM((UNIT_BINS, 1, columns), F32),
            pltpu.VMEM((UNIT_BINS, 1, columns), F32),
        ],
    )(*args)


def freq_stage(rows, match, value_t):
    parts, frames, each, width = rows.shape
    bins = parts * each
    return call(
        freq_kernel,
        "freq_stage",
        5,
        in_specs=[full(rows), full(match), full(value_t)],
        out_specs=full(rows),
        out_shape=jax.ShapeDtypeStruct(rows.shape, BF16),
        scratch_shapes=[
            pltpu.VMEM((frames, bins, width), BF16),
            pltpu.VMEM((frames, width, bins), BF16),
            pltpu.VMEM((HEADS * bins, bins), F32),
            pltpu.VMEM((HEADS * bins, bins), BF16),
            pltpu.VMEM((HEADS, bins), F32),
        ],
    )(rows, match, value_t)


def add_branch(base, mixed, weight):
    return (base.astype(F32) + dot_nn(mixed, weight)).astype(BF16)


def feed_forward(after_freq, mlp_gain, mlp_up, mlp_down):
    hidden = jax.nn.gelu(dot_nn(layer_norm(after_freq, mlp_gain), mlp_up)).astype(BF16)
    return add_branch(after_freq, hidden, mlp_down)


def key_bias(segment_ids, active, count):
    frames = segment_ids.shape[0]
    span = count + 2 * HALO
    start = lax.axis_index("tm") * count
    seg_query = lax.dynamic_slice_in_dim(segment_ids, start, count, 0)
    seg_key = lax.dynamic_slice_in_dim(jnp.pad(segment_ids, HALO, constant_values=-1), start, span, 0)
    act_key = lax.dynamic_slice_in_dim(jnp.pad(active, HALO), start, span, 0)
    pos_key = start - HALO + jnp.arange(span, dtype=jnp.int32)
    pos_query = start + jnp.arange(count, dtype=jnp.int32)
    inside = (pos_key >= 0) & (pos_key < frames)
    allowed = (
        inside[:, None]
        & (seg_query[None, :] == seg_key[:, None])
        & ((act_key[:, None] == 1) | (pos_query[None, :] == pos_key[:, None]))
    )
    return jnp.where(allowed, 0.0, NEG).astype(F32)


def per_device(
    spec,
    segment_ids,
    active,
    time_gain,
    time_match,
    time_value,
    time_out,
    freq_gain,
    freq_match,
    freq_value,
    freq_out,
    mlp_gain,
    mlp_up,
    mlp_down,
):
    bins, count, width = spec.shape
    peers = lax.axis_size("tm")
    parts = lax.axis_size("freq")
    up = [(i, i + 1) for i in range(peers - 1)]
    down = [(j, i) for i, j in up]
    before = lax.ppermute(spec[:, count - HALO :], "tm", up)
    after = lax.ppermute(spec[:, :HALO], "tm", down)
    bias = key_bias(segment_ids, active, count)
    side_bias = jnp.concatenate([bias[:HALO], bias[HALO + count :]], 0)
    time_value_t, freq_value_t = time_value.T, freq_value.T
    partial = own_stage(spec, bias[HALO : HALO + count], time_gain[None], time_match, time_value_t)
    base, *sent = halo_stage(
        parts, before, spec, after, side_bias, time_gain[None], time_match, time_value_t, time_out, freq_gain[None],
        partial,
    )
    base, freq_value_t, *sent = lax.optimization_barrier((jnp.swapaxes(base, 0, 1), freq_value_t, *sent))
    gathered = [exchange(s) for s in sent]
    returned = [exchange(freq_stage(g, freq_match, freq_value_t)) for g in gathered]
    mixed = returned[0].reshape(count, bins, width)
    after_freq = add_branch(base, mixed, freq_out)
    result = lax.optimization_barrier(feed_forward(after_freq, mlp_gain, mlp_up, mlp_down))
    return jnp.swapaxes(result, 0, 1)


def exchange(array):
    return lax.all_to_all(array, "freq", split_axis=0, concat_axis=0, tiled=True)


def solution(mesh):
    placed = (P("freq", "tm", None),) + (P(),) * 13
    return jax.shard_map(
        per_device, mesh=mesh, in_specs=placed, out_specs=P("freq", "tm", None), check_vma=False
    )
```
